768 devices in a mesh: dp: 192 (over x, y_lo, z, core), pipe: 4 (over y_hi).
Axes of the slice: x: 4, y: 8 (y_hi: 4, y_lo: 2; y = y_hi * 2 + y_lo), z: 12, core: 2. Of those that a mesh axis runs over, the one named last changes fastest.
Arguments:
- acts: bfloat16 [4, 2, 12288, 4224], P('pipe', None, 'dp'), may hold values from -6 to 6
- out_grad: bfloat16 [2, 12288, 4224], P(None, 'dp'), may hold values from -6 to 6
- params: bfloat16 [4, 768, 4224], P('pipe'), may hold values from -0.09375 to 0.09375
- moment: float32 [4, 1081344], P('pipe', 'dp'), may hold values from -2 to 2
- second: float32 [4, 1081344], P('pipe', 'dp'), may hold values from 0.0001 to 0.01
Outputs:
- in_grad: bfloat16 [4, 2, 12288, 4224], P('pipe', None, 'dp')
- new_moment: float32 [4, 1081344], P('pipe', 'dp')
- new_second: float32 [4, 1081344], P('pipe', 'dp')
- update: float32 [4, 1081344], P('pipe', 'dp')
The draws below stay inside these ranges and needn't reach their ends.
All inputs are finite; a program needn't handle non-finite values.
Results may differ from the reference program's by a relative error of at most 0.0056.
Values may be sent and summed in bfloat16 or wider, within the bound.
No kernel may reach another device: no remote copies, remote signals or barrier semaphores. Data moves between devices by JAX's collectives and lax.ppermute only.
A program may use at most 64 MiB of HBM per device.

```python
import math
import jax
import jax.numpy as jnp

D = 4224
BLOCK = 256
MICRO = 2
TOKENS = 12288
SECTIONS = 4


def block_levels(own_key, shape, cuts, low, largest):
    gain = 1.0
    for axis_at, blocks in cuts:
        draws = jax.random.uniform(jax.random.fold_in(jax.random.fold_in(own_key, 6), axis_at), (blocks,), jnp.float32, low / len(cuts), largest / len(cuts))
        gain = gain * jnp.repeat(jnp.exp(draws), shape[axis_at] // blocks).reshape((-1,) + (1,) * (len(shape) - 1 - axis_at))
    return gain


def noise(stream_key, dims, spread, limit, shards=(), dtype=jnp.bfloat16):
    array = jax.random.normal(stream_key, dims, jnp.float32) * spread
    if len(shards) > 0:
        array = block_levels(stream_key, dims, shards, -0.22, 0.18) * array
    return jnp.clip(array, min=-limit, max=limit).astype(dtype)


def setup_inputs(seed: int = 0) -> dict:
    splits = jax.random.split(jax.random.key(seed), 6)
    acts = noise(splits[0], (SECTIONS, MICRO, TOKENS, D), 1.0, 6.0, ((0, 4), (2, 192)))
    out_grad = noise(splits[1], (MICRO, TOKENS, D), 1.0, 6.0, ((1, 192),))
    params = noise(splits[2], (SECTIONS, 3 * BLOCK, D), D ** -0.5, 0.09375, ((0, 4),))
    moment = noise(splits[3], (SECTIONS, BLOCK * D), 0.3, 2.0, ((0, 4), (1, 192)), jnp.float32)
    second = jnp.clip(jnp.exp(math.log(0.01) - 4.6051702 * jax.random.uniform(splits[4], (SECTIONS, BLOCK * D), jnp.float32) ** block_levels(splits[4], (SECTIONS, BLOCK * D), ((0, 4), (1, 192)), -0.2, 0.2)), 0.0001, 0.01)
    return {"acts": acts, "out_grad": out_grad, "params": params, "moment": moment, "second": second}


def section_back(inputs, grad_rows, weights):
    block_size = weights.shape[0] // 3
    weights_in = weights[:2 * block_size]
    weights_down = weights[2 * block_size:]
    gate_up = jnp.dot(inputs, weights_in.T, preferred_element_type=jnp.float32)
    gate_values = gate_up[:, :block_size]
    up_values = gate_up[:, block_size:]
    sigmoid_gate = jax.nn.sigmoid(gate_values)
    activated = gate_values * sigmoid_gate
    d_hidden = jnp.dot(grad_rows, weights_down.T, preferred_element_type=jnp.float32)
    d_gate = d_hidden * up_values * sigmoid_gate * (1.0 + gate_values * (1.0 - sigmoid_gate))
    d_up = d_hidden * activated
    d_gate_up = jnp.concatenate([d_gate, d_up], axis=1).astype(jnp.bfloat16)
    hidden = (activated * up_values).astype(jnp.bfloat16)
    passed = grad_rows.astype(jnp.float32) + jnp.dot(d_gate_up, weights_in, preferred_element_type=jnp.float32)
    return (passed.astype(jnp.bfloat16), hidden)

def reference(acts, out_grad, params, moment, second):
    section_count = acts.shape[0]
    micro_count = acts.shape[1]
    grad_scale = float(micro_count * acts.shape[2]) ** (-0.5)
    block_size = params.shape[1] // 3
    totals = [jnp.zeros((block_size, params.shape[2]), jnp.float32) for _ in range(section_count)]
    passed_all = [[None] * micro_count for _ in range(section_count)]
    for micro_index in range(micro_count):
        grad_rows = out_grad[micro_index]
        for section_index in reversed(range(section_count)):
            inputs = acts[section_index, micro_index]
            passed, hidden = section_back(inputs, grad_rows, params[section_index])
            term = jnp.dot(hidden.T, grad_rows, preferred_element_type=jnp.float32)
            totals[section_index] = totals[section_index] + term
            passed_all[section_index][micro_index] = passed
            grad_rows = passed
    in_grad = jnp.stack([jnp.stack(passed_all[section_index]) for section_index in range(section_count)])
    gradient = jnp.stack(totals).reshape(section_count, -1) * grad_scale
    new_moment = 0.9 * moment + 0.1 * gradient
    new_second = 0.999 * second + 0.001 * gradient * gradient
    update = new_moment / (1.0 - 0.9 ** 10) / (jnp.sqrt(new_second / (1.0 - 0.999 ** 10)) + 1e-08)
    return (in_grad, new_moment, new_second, update)
```

```python
import jax
import jax.numpy as jnp
from jax import lax
from jax.sharding import Mesh, PartitionSpec as P

CHUNKS = 4
DP = ("x", "yl", "z", "core")


def shifted(value, rows, steps, lead, total):
    width = value.shape[1]
    pad = jnp.zeros((lead * rows, width), value.dtype)
    padded = jnp.concatenate([pad, value, pad], axis=0)
    return lax.dynamic_slice(padded, (steps * rows, 0), (total * rows, width))


def reduce_rows(term):
    core = lax.axis_index("core")
    shares = term.reshape(96, 2, -1, 128)
    mine = jnp.where(core == 0, shares[:, 0], shares[:, 1])
    other = jnp.where(core == 0, shares[:, 1], shares[:, 0]).astype(jnp.bfloat16)
    got = lax.ppermute(other, "core", [(0, 1), (1, 0)])
    half = (mine + got.astype(jnp.float32)).astype(jnp.bfloat16)
    got = lax.all_to_all(half, ("x", "yl", "z"), 0, 0, tiled=True)
    return jnp.sum(got.astype(jnp.float32), axis=0).reshape(-1)


def local(acts, out_grad, params, moment, second):
    sections = lax.axis_size("pipe")
    section = lax.axis_index("pipe")
    width = acts.shape[-1]
    inputs = acts.reshape(-1, width)
    top = out_grad.reshape(-1, width)
    tokens = inputs.shape[0]
    rows = tokens // CHUNKS
    lead = sections - 1
    ticks = CHUNKS + lead
    block = params.shape[1] // 3
    weights_in = params[0, : 2 * block]
    weights_down = params[0, 2 * block :]
    gate_up = lax.dot_general(
        inputs, weights_in, (((1,), (1,)), ((), ())), preferred_element_type=jnp.float32
    )
    gate = gate_up[:, :block]
    up = gate_up[:, block:]
    sg = jax.nn.sigmoid(gate)
    activated = gate * sg
    factors = jnp.concatenate([up * sg * (1.0 + gate * (1.0 - sg)), activated], axis=1)
    hidden = (activated * up).astype(jnp.bfloat16)
    factors = shifted(factors, rows, section, lead, ticks)

    incoming = jnp.zeros((rows, width), jnp.bfloat16)
    grads = []
    passes = []
    for tick in range(ticks):
        grad = incoming
        if tick < CHUNKS:
            grad = jnp.where(section == lead, top[tick * rows : (tick + 1) * rows], incoming)
        d_hidden = lax.dot_general(
            grad, weights_down, (((1,), (1,)), ((), ())), preferred_element_type=jnp.float32
        )
        part = factors[tick * rows : (tick + 1) * rows]
        d_gate_up = (jnp.concatenate([d_hidden, d_hidden], axis=1) * part).astype(jnp.bfloat16)
        passed = grad.astype(jnp.float32) + jnp.dot(
            d_gate_up, weights_in, preferred_element_type=jnp.float32
        )
        passed = passed.astype(jnp.bfloat16)
        grads.append(grad)
        passes.append(passed)
        if tick + 1 < ticks:
            incoming = lax.ppermute(passed, "pipe", [(s, s - 1) for s in range(1, sections)])
    first = (lead - section) * rows
    arrived = lax.dynamic_slice(jnp.concatenate(grads, axis=0), (first, 0), (tokens, width))
    in_grads = lax.dynamic_slice(jnp.concatenate(passes, axis=0), (first, 0), (tokens, width))
    term = lax.dot_general(
        hidden, arrived, (((0,), (0,)), ((), ())), preferred_element_type=jnp.float32
    )
    total = tokens * lax.axis_size(DP)
    gradient = reduce_rows(term) * float(total) ** (-0.5)
    new_moment = 0.9 * moment[0] + 0.1 * gradient
    new_second = 0.999 * second[0] + 0.001 * gradient * gradient
    update = new_moment / (1.0 - 0.9**10) / (jnp.sqrt(new_second / (1.0 - 0.999**10)) + 1e-08)
    return (in_grads.reshape(acts.shape), new_moment[None], new_second[None], update[None])


def solution(mesh):
    fine = Mesh(mesh.devices.reshape(4, 2, 12, 2, 4), DP + ("pipe",))
    placed = (
        P("pipe", None, DP, None),
        P(None, DP, None),
        P("pipe", None, None),
        P("pipe", DP),
        P("pipe", DP),
    )
    return jax.shard_map(
        local,
        mesh=fine,
        in_specs=placed,
        out_specs=(P("pipe", None, DP, None), P("pipe", DP), P("pipe", DP), P("pipe", DP)),
        check_vma=False,
    )
```

```python
import jax
import jax.numpy as jnp
from jax import lax
from jax.sharding import Mesh, PartitionSpec as P

CHUNKS = 4
DP = ("x", "yl", "z", "core")
SIDE = ("x", "core")
F32 = jnp.float32
BF16 = jnp.bfloat16


def rows_dot(left, right):
    return lax.dot_general(left, right, (((0,), (0,)), ((), ())), preferred_element_type=F32)


def cols_dot(left, right):
    return lax.dot_general(left, right, (((1,), (1,)), ((), ())), preferred_element_type=F32)


def spread(value, places):
    shape = (value.shape[1], places * 2)
    have = lax.broadcasted_iota(jnp.int32, shape, 0)
    col = lax.broadcasted_iota(jnp.int32, shape, 1)
    place = col // 2
    want = (place // 3) * 4 + place % 3 + col % 2
    return jnp.dot(value, (have == want).astype(BF16), preferred_element_type=F32).astype(BF16)


def to_side(rows):
    count = lax.axis_size(SIDE)
    parts = rows.reshape(rows.shape[0], count, -1).transpose(1, 0, 2)
    parts = lax.all_to_all(parts, SIDE, 0, 0, tiled=True)
    return parts.reshape(-1, parts.shape[2])


def step(acts, out_grad, params, moment, second):
    sections = lax.axis_size("pipe")
    section = lax.axis_index("pipe")
    places = lax.axis_size(DP)
    side = lax.axis_size(SIDE)
    width = acts.shape[-1]
    inputs = acts.reshape(-1, width)
    top = out_grad.reshape(-1, width)
    tokens = inputs.shape[0]
    rows = tokens // CHUNKS
    lead = sections - 1
    ticks = CHUNKS + lead
    block = params.shape[1] // 3
    weights_in = params[0, : 2 * block]
    weights_down = params[0, 2 * block :]
    gate_up = cols_dot(inputs, weights_in)
    gate = gate_up[:, :block]
    up = gate_up[:, block:]
    sg = jax.nn.sigmoid(gate)
    activated = gate * sg
    factors = jnp.concatenate([up * sg * (1.0 + gate * (1.0 - sg)), activated], axis=1)
    hidden = (activated * up).astype(BF16)
    pad = jnp.zeros((lead * rows, 2 * block), F32)
    factors = lax.dynamic_slice(
        jnp.concatenate([pad, factors, pad], axis=0),
        (section * rows, 0),
        (ticks * rows, 2 * block),
    )
    down = [(s, s - 1) for s in range(1, sections)]
    most = tokens - rows

    def own(values, chunk, among=sections):
        value = values[chunk]
        for behind in range(1, among):
            value = jnp.where(section == lead - behind, values[chunk + behind], value)
        return value

    moved = []
    grads = []
    passes = []
    for tick in range(ticks):
        grad = jnp.zeros((rows, width), BF16) if tick == 0 else moved[tick - 1]
        if tick < CHUNKS:
            grad = jnp.where(section == lead, top[tick * rows : (tick + 1) * rows], grad)
        d_hidden = cols_dot(grad, weights_down)
        part = factors[tick * rows : (tick + 1) * rows]
        d_gate_up = (jnp.concatenate([d_hidden, d_hidden], axis=1) * part).astype(BF16)
        passed = grad.astype(F32) + jnp.dot(d_gate_up, weights_in, preferred_element_type=F32)
        passed = passed.astype(BF16)
        grads.append(grad)
        passes.append(passed)
        if tick + 1 < ticks:
            moved.append(lax.ppermute(passed, "pipe", down))
        if tick == 0:
            hidden, _ = lax.optimization_barrier((hidden, passed))
            copies = jnp.broadcast_to(hidden[None], (side,) + hidden.shape)
            hidden = lax.all_to_all(copies, SIDE, 0, 0, tiled=True)
            hidden = spread(hidden.reshape(-1, block), places).reshape(side, tokens, -1)
        if tick + 2 == ticks:
            arrived = jnp.concatenate([own(grads, chunk) for chunk in range(CHUNKS - 1)], axis=0)
            last = own(grads, CHUNKS - 1, lead)
            arrived, last = lax.optimization_barrier((arrived, last))
            terms = rows_dot(hidden[:, :most].reshape(side * most, -1), to_side(arrived))
    arrived = jnp.where(section == 0, grads[-1], last)
    terms = terms + rows_dot(hidden[:, most:].reshape(side * rows, -1), to_side(arrived))
    in_grads = jnp.concatenate([own(passes, chunk) for chunk in range(CHUNKS)], axis=0)

    terms = terms.astype(BF16).reshape(places, 2, -1)
    terms = lax.all_to_all(terms, DP, 0, 0, tiled=True)
    sizes = tuple(lax.axis_size(name) for name in DP)
    summed = jnp.sum(terms.astype(F32).reshape(sizes + terms.shape[1:]), axis=(1, 2))
    summed = summed.transpose(2, 0, 1, 3).reshape(-1)
    start = lax.rem(lax.axis_index(DP), 3) * (width // 3)
    summed = lax.dynamic_slice(summed, (start,), (moment.shape[1],))

    gradient = summed * float(tokens * places) ** (-0.5)
    new_moment = 0.9 * moment[0] + 0.1 * gradient
    new_second = 0.999 * second[0] + 0.001 * gradient * gradient
    update = new_moment / (1.0 - 0.9**10) / (jnp.sqrt(new_second / (1.0 - 0.999**10)) + 1e-08)
    return (in_grads.reshape(acts.shape), new_moment[None], new_second[None], update[None])


def solution(mesh):
    fine = Mesh(mesh.devices.reshape(4, 2, 12, 2, 4), DP + ("pipe",))
    placed = (
        P("pipe", None, DP, None),
        P(None, DP, None),
        P("pipe", None, None),
        P("pipe", DP),
        P("pipe", DP),
    )
    return jax.shard_map(
        step,
        mesh=fine,
        in_specs=placed,
        out_specs=(P("pipe", None, DP, None), P("pipe", DP), P("pipe", DP), P("pipe", DP)),
        check_vma=False,
    )
```

```python
import jax
import jax.numpy as jnp
from jax import lax
from jax.sharding import Mesh, PartitionSpec as P

CHUNKS = 4
DP = ("x", "yl", "z", "core")
SIDE = ("x", "core")
F32 = jnp.float32
BF16 = jnp.bfloat16


def rows_dot(left, right):
    return lax.dot_general(left, right, (((0,), (0,)), ((), ())), preferred_element_type=F32)


def cols_dot(left, right):
    return lax.dot_general(left, right, (((1,), (1,)), ((), ())), preferred_element_type=F32)


def spread(value, places):
    shape = (value.shape[1], places * 2)
    have = lax.broadcasted_iota(jnp.int32, shape, 0)
    col = lax.broadcasted_iota(jnp.int32, shape, 1)
    place = col // 2
    want = (place // 3) * 4 + place % 3 + col % 2
    return jnp.dot(value, (have == want).astype(BF16), preferred_element_type=F32).astype(BF16)


def to_side(rows):
    count = lax.axis_size(SIDE)
    parts = rows.reshape(rows.shape[0], count, -1).transpose(1, 0, 2)
    parts = lax.all_to_all(parts, SIDE, 0, 0, tiled=True)
    return parts.reshape(-1, parts.shape[2])


def step(acts, out_grad, params, moment, second):
    sections = lax.axis_size("pipe")
    section = lax.axis_index("pipe")
    places = lax.axis_size(DP)
    side = lax.axis_size(SIDE)
    width = acts.shape[-1]
    first_chunk = (section * (acts.shape[1] * acts.shape[2] // CHUNKS)).astype(jnp.uint32)
    third = (lax.rem(lax.axis_index(DP), 3) * (width // 3)).astype(jnp.uint32)
    is_section = [section == at for at in range(sections)]
    acts, first_chunk, third, is_section = lax.optimization_barrier(
        (acts, first_chunk, third, is_section)
    )
    inputs = acts.reshape(-1, width)
    top = out_grad.reshape(-1, width)
    tokens = inputs.shape[0]
    rows = tokens // CHUNKS
    lead = sections - 1
    ticks = CHUNKS + lead
    block = params.shape[1] // 3
    weights_in = params[0, : 2 * block]
    weights_down = params[0, 2 * block :]
    gate_up = cols_dot(inputs, weights_in)
    gate = gate_up[:, :block]
    up = gate_up[:, block:]
    sg = jax.nn.sigmoid(gate)
    activated = gate * sg
    factors = jnp.concatenate([up * sg * (1.0 + gate * (1.0 - sg)), activated], axis=1)
    hidden = (activated * up).astype(BF16)
    pad = jnp.zeros((lead * rows, 2 * block), F32)
    factors = lax.dynamic_slice(
        jnp.concatenate([pad, factors, pad], axis=0),
        (first_chunk, jnp.uint32(0)),
        (ticks * rows, 2 * block),
    )
    copies = jnp.broadcast_to(hidden[None], (side,) + hidden.shape)
    hidden = lax.all_to_all(copies, SIDE, 0, 0, tiled=True)
    hidden = spread(hidden.reshape(-1, block), places).reshape(side, tokens, -1)
    down = [(s, s - 1) for s in range(1, sections)]
    early = CHUNKS - 2
    cuts = (0, early * rows, (early + 1) * rows, tokens)

    def own(values, chunk, among=sections):
        value = values[chunk]
        for behind in range(1, among):
            value = jnp.where(is_section[lead - behind], values[chunk + behind], value)
        return value

    moved = []
    grads = []
    passes = []
    for tick in range(ticks):
        grad = jnp.zeros((rows, width), BF16) if tick == 0 else moved[tick - 1]
        if tick < CHUNKS:
            grad = jnp.where(is_section[lead], top[tick * rows : (tick + 1) * rows], grad)
        d_hidden = cols_dot(grad, weights_down)
        part = factors[tick * rows : (tick + 1) * rows]
        d_gate_up = (jnp.concatenate([d_hidden, d_hidden], axis=1) * part).astype(BF16)
        passed = grad.astype(F32) + jnp.dot(d_gate_up, weights_in, preferred_element_type=F32)
        passed = passed.astype(BF16)
        grads.append(grad)
        passes.append(passed)
        if tick + 1 < ticks:
            moved.append(lax.ppermute(passed, "pipe", down))
        if tick == ticks - 3:
            arrived = jnp.concatenate([own(grads, chunk) for chunk in range(early)], axis=0)
            after = (own(grads, early, lead), own(grads, early + 1, lead - 1))
            arrived, after = lax.optimization_barrier((arrived, after))
            sides = [to_side(arrived)]
        if tick == ticks - 2:
            arrived = jnp.where(is_section[0], grads[-1], after[0])
            after = jnp.where(is_section[1], grads[-1], after[1])
            arrived, after = lax.optimization_barrier((arrived, after))
            sides.append(to_side(arrived))
    arrived = jnp.where(is_section[0], grads[-1], after)
    sides.append(to_side(arrived))
    passes, sides = lax.optimization_barrier((passes, sides))
    terms = 0.0
    for begin, end, rows_of_side in zip(cuts[:-1], cuts[1:], sides):
        terms = terms + rows_dot(
            hidden[:, begin:end].reshape(side * (end - begin), -1), rows_of_side
        )
    in_grads = jnp.concatenate([own(passes, chunk) for chunk in range(CHUNKS)], axis=0)

    terms = terms.astype(BF16).reshape(places, 2, -1)
    terms = lax.all_to_all(terms, DP, 0, 0, tiled=True)
    sizes = tuple(lax.axis_size(name) for name in DP)
    summed = jnp.sum(terms.astype(F32).reshape(sizes + terms.shape[1:]), axis=(1, 2))
    summed = summed.transpose(2, 0, 1, 3).reshape(-1)
    summed = lax.dynamic_slice(summed, (third,), (moment.shape[1],))

    gradient = summed * float(tokens * places) ** (-0.5)
    new_moment = 0.9 * moment[0] + 0.1 * gradient
    new_second = 0.999 * second[0] + 0.001 * gradient * gradient
    update = new_moment / (1.0 - 0.9**10) / (jnp.sqrt(new_second / (1.0 - 0.999**10)) + 1e-08)
    return (in_grads.reshape(acts.shape), new_moment[None], new_second[None], update[None])


def solution(mesh):
    fine = Mesh(mesh.devices.reshape(4, 2, 12, 2, 4), DP + ("pipe",))
    placed = (
        P("pipe", None, DP, None),
        P(None, DP, None),
        P("pipe", None, None),
        P("pipe", DP),
        P("pipe", DP),
    )
    return jax.shard_map(
        step,
        mesh=fine,
        in_specs=placed,
        out_specs=(P("pipe", None, DP, None), P("pipe", DP), P("pipe", DP), P("pipe", DP)),
        check_vma=False,
    )
```

```python
import jax
import jax.numpy as jnp
from jax import lax
from jax.sharding import Mesh, PartitionSpec as P


CHUNKS = 8
DEPTH = 2
DP = ("x", "yl", "z", "core")
SIDE = ("x", "core")
F32 = jnp.float32
BF16 = jnp.bfloat16


def rows_dot(left, right):
    return lax.dot_general(left, right, (((0,), (0,)), ((), ())), preferred_element_type=F32)


def cols_dot(left, right):
    return lax.dot_general(left, right, (((1,), (1,)), ((), ())), preferred_element_type=F32)


def to_side(rows):
    count = lax.axis_size(SIDE)
    parts = rows.reshape(rows.shape[0], 3, count, -1).transpose(2, 0, 1, 3)
    parts = parts.reshape(count, rows.shape[0], -1)
    parts = lax.all_to_all(parts, SIDE, 0, 0, tiled=True)
    return parts.reshape(-1, parts.shape[2])


def step(acts, out_grad, params, moment, second):
    sections = lax.axis_size("pipe")
    section = lax.axis_index("pipe")
    places = lax.axis_size(DP)
    side = lax.axis_size(SIDE)
    width = acts.shape[-1]
    tokens = acts.shape[1] * acts.shape[2]
    rows = tokens // CHUNKS
    lead = sections - 1
    ticks = CHUNKS + DEPTH * lead
    first_chunk = (section * (DEPTH * rows)).astype(jnp.uint32)
    is_section = [section == at for at in range(sections)]
    acts, first_chunk, is_section = lax.optimization_barrier((acts, first_chunk, is_section))
    inputs = acts.reshape(-1, width)
    top = out_grad.reshape(-1, width)
    block = params.shape[1] // 3
    weights_in = params[0, : 2 * block]
    weights_down = params[0, 2 * block :]
    gate_up = cols_dot(inputs, weights_in)
    gate = gate_up[:, :block]
    up = gate_up[:, block:]
    sg = jax.nn.sigmoid(gate)
    activated = gate * sg
    factors = jnp.concatenate([up * sg * (1.0 + gate * (1.0 - sg)), activated], axis=1)
    hidden = (activated * up).astype(BF16)
    pad = jnp.zeros((DEPTH * lead * rows, 2 * block), F32)
    factors = lax.dynamic_slice(
        jnp.concatenate([pad, factors, pad], axis=0),
        (first_chunk, jnp.uint32(0)),
        (ticks * rows, 2 * block),
    )
    copies = jnp.broadcast_to(hidden[None], (side,) + hidden.shape)
    hidden = lax.all_to_all(copies, SIDE, 0, 0, tiled=True)
    top = jnp.where(is_section[lead], top, 0)
    tops = lax.optimization_barrier(
        [top[chunk * rows : (chunk + 1) * rows] for chunk in range(CHUNKS)]
    )
    down = [(s, s - 1) for s in range(1, sections)]
    cuts = (0, CHUNKS - 2, CHUNKS)

    def own(values, count):
        chunks = []
        for chunk in range(count):
            value = values[chunk]
            for behind in range(1, sections):
                value = jnp.where(is_section[lead - behind], values[chunk + DEPTH * behind], value)
            chunks.append(value)
        return jnp.concatenate(chunks, axis=0)

    moved = []
    grads = []
    passes = []
    sides = []
    for tick in range(ticks):
        grad = None if tick < DEPTH else moved[tick - DEPTH]
        if tick < CHUNKS:
            grad = tops[tick] if grad is None else grad + tops[tick]
        grads.append(grad)
        d_hidden = cols_dot(grad, weights_down)
        part = factors[tick * rows : (tick + 1) * rows]
        d_gate_up = (jnp.concatenate([d_hidden, d_hidden], axis=1) * part).astype(BF16)
        passed = grad.astype(F32) + jnp.dot(d_gate_up, weights_in, preferred_element_type=F32)
        passed = passed.astype(BF16)
        passes.append(passed)
        if tick + DEPTH < ticks:
            moved.append(lax.ppermute(passed, "pipe", down))
        done = tick + 1 - DEPTH * lead
        if done in cuts[1:]:
            begin = cuts[len(sides)]
            seen, _ = lax.optimization_barrier((grads[begin:], passed if done < CHUNKS else grad))
            arrived = own(seen, done - begin)
            sides.append(to_side(arrived))

    passes, sides = lax.optimization_barrier((passes, sides))
    terms = 0.0
    for begin, end, rows_of_side in zip(cuts[:-1], cuts[1:], sides):
        part = hidden[:, begin * rows : end * rows].reshape(-1, block)
        terms = terms + rows_dot(part, rows_of_side)

    in_grads = own(passes, CHUNKS)

    terms = terms.astype(BF16).reshape(places, 2, -1)
    terms = lax.all_to_all(terms, DP, 0, 0, tiled=True)
    sizes = tuple(lax.axis_size(name) for name in DP)
    summed = jnp.sum(terms.astype(F32).reshape(sizes + terms.shape[1:]), axis=(1, 2))
    summed = summed.reshape(side, 4, -1).transpose(1, 0, 2).reshape(-1)

    gradient = summed * float(tokens * places) ** (-0.5)
    new_moment = 0.9 * moment[0] + 0.1 * gradient
    new_second = 0.999 * second[0] + 0.001 * gradient * gradient
    update = new_moment / (1.0 - 0.9**10) / (jnp.sqrt(new_second / (1.0 - 0.999**10)) + 1e-08)
    return (in_grads.reshape(acts.shape), new_moment[None], new_second[None], update[None])


def solution(mesh):
    fine = Mesh(mesh.devices.reshape(4, 2, 12, 2, 4), DP + ("pipe",))
    placed = (
        P("pipe", None, DP, None),
        P(None, DP, None),
        P("pipe", None, None),
        P("pipe", DP),
        P("pipe", DP),
    )
    return jax.shard_map(
        step,
        mesh=fine,
        in_specs=placed,
        out_specs=(P("pipe", None, DP, None), P("pipe", DP), P("pipe", DP), P("pipe", DP)),
        check_vma=False,
    )
```

```python
import jax
import jax.numpy as jnp
from jax import lax
from jax.sharding import Mesh, PartitionSpec as P


CHUNKS = 8
DEPTH = 2
DP = ("x", "yl", "z", "core")
SIDE = ("x", "core")
F32 = jnp.float32
BF16 = jnp.bfloat16


def rows_dot(left, right):
    return lax.dot_general(left, right, (((0,), (0,)), ((), ())), preferred_element_type=F32)


def cols_dot(left, right):
    return lax.dot_general(left, right, (((1,), (1,)), ((), ())), preferred_element_type=F32)


def side_parts(rows, count):
    parts = rows.reshape(rows.shape[0], 3, count, -1).transpose(2, 0, 1, 3)
    return parts.reshape(count, rows.shape[0], -1)


def step(acts, out_grad, params, moment, second):
    sections = lax.axis_size("pipe")
    section = lax.axis_index("pipe")
    places = lax.axis_size(DP)
    side = lax.axis_size(SIDE)
    width = acts.shape[-1]
    tokens = acts.shape[1] * acts.shape[2]
    rows = tokens // CHUNKS
    lead = sections - 1
    ticks = CHUNKS + DEPTH * lead
    first_chunk = (section * (DEPTH * rows)).astype(jnp.uint32)
    is_section = [section == at for at in range(sections)]
    acts, first_chunk, is_section = lax.optimization_barrier((acts, first_chunk, is_section))
    inputs = acts.reshape(-1, width)
    top = out_grad.reshape(-1, width)
    block = params.shape[1] // 3
    weights_in = params[0, : 2 * block]
    weights_down = params[0, 2 * block :]
    gate_up = cols_dot(inputs, weights_in)
    gate = gate_up[:, :block]
    up = gate_up[:, block:]
    sg = jax.nn.sigmoid(gate)
    activated = gate * sg
    factors = jnp.concatenate([up * sg * (1.0 + gate * (1.0 - sg)), activated], axis=1)
    hidden = (activated * up).astype(BF16)
    pad = jnp.zeros((DEPTH * lead * rows, 2 * block), F32)
    factors = lax.dynamic_slice(
        jnp.concatenate([pad, factors, pad], axis=0),
        (first_chunk, jnp.uint32(0)),
        (ticks * rows, 2 * block),
    )
    factors = lax.optimization_barrier(
        [factors[tick * rows : (tick + 1) * rows] for tick in range(ticks)]
    )
    copies = jnp.broadcast_to(hidden[None], (side,) + hidden.shape)
    hidden = lax.all_to_all(copies, SIDE, 0, 0, tiled=True)
    top = jnp.where(is_section[lead], top, 0)
    tops = lax.optimization_barrier(
        [top[chunk * rows : (chunk + 1) * rows] for chunk in range(CHUNKS)]
    )
    down = [(s, s - 1) for s in range(1, sections)]
    def own(values, count):
        chunks = []
        for chunk in range(count):
            value = values[chunk]
            for behind in range(1, sections):
                value = jnp.where(is_section[lead - behind], values[chunk + DEPTH * behind], value)
            chunks.append(value)
        return jnp.concatenate(chunks, axis=0)

    moved = []
    grads = []
    passes = []
    parts = []
    for tick in range(ticks):
        grad = None if tick < DEPTH else moved[tick - DEPTH]
        if tick < CHUNKS:
            grad = tops[tick] if grad is None else grad + tops[tick]
        grads.append(grad)
        d_hidden = cols_dot(grad, weights_down)
        d_gate_up = jnp.concatenate([d_hidden, d_hidden], axis=1) * factors[tick]
        d_gate_up = d_gate_up.astype(BF16)
        passed = grad.astype(F32) + jnp.dot(d_gate_up, weights_in, preferred_element_type=F32)
        passed = passed.astype(BF16)
        passes.append(passed)
        if tick + DEPTH < ticks:
            moved.append(lax.ppermute(passed, "pipe", down))
        done = tick + 1 - DEPTH * lead
        if done == CHUNKS - DEPTH or done == CHUNKS:
            begin = len(parts) * (CHUNKS - DEPTH)
            seen, _ = lax.optimization_barrier((grads[begin:], passed if begin == 0 else grad))
            parts.append(side_parts(own(seen, done - begin), side))
    arrived = lax.all_to_all(jnp.concatenate(parts, axis=1), SIDE, 0, 0, tiled=True)
    passes, arrived = lax.optimization_barrier((passes, arrived))
    terms = rows_dot(hidden.reshape(-1, block), arrived.reshape(-1, arrived.shape[2]))

    in_grads = own(passes, CHUNKS)

    terms = terms.astype(BF16).reshape(places, 2, -1)
    terms = lax.all_to_all(terms, DP, 0, 0, tiled=True)
    sizes = tuple(lax.axis_size(name) for name in DP)
    summed = jnp.sum(terms.astype(F32).reshape(sizes + terms.shape[1:]), axis=(1, 2))
    summed = summed.reshape(side, 4, -1).transpose(1, 0, 2).reshape(-1)

    gradient = summed * float(tokens * places) ** (-0.5)
    new_moment = 0.9 * moment[0] + 0.1 * gradient
    new_second = 0.999 * second[0] + 0.001 * gradient * gradient
    update = new_moment / (1.0 - 0.9**10) / (jnp.sqrt(new_second / (1.0 - 0.999**10)) + 1e-08)
    return (in_grads.reshape(acts.shape), new_moment[None], new_second[None], update[None])


def solution(mesh):
    fine = Mesh(mesh.devices.reshape(4, 2, 12, 2, 4), DP + ("pipe",))
    placed = (
        P("pipe", None, DP, None),
        P(None, DP, None),
        P("pipe", None, None),
        P("pipe", DP),
        P("pipe", DP),
    )
    return jax.shard_map(
        step,
        mesh=fine,
        in_specs=placed,
        out_specs=(P("pipe", None, DP, None), P("pipe", DP), P("pipe", DP), P("pipe", DP)),
        check_vma=False,
    )
```

```python
import jax
import jax.numpy as jnp
from jax import lax
from jax.experimental import pallas as pl
from jax.experimental.pallas import tpu as pltpu
from jax.sharding import Mesh, PartitionSpec as P


CHUNKS = 8
DEPTH = 2
DP = ("x", "yl", "z", "core")
SIDE = ("x", "core")
F32 = jnp.float32
BF16 = jnp.bfloat16


def rows_dot(left, right):
    return lax.dot_general(left, right, (((0,), (0,)), ((), ())), preferred_element_type=F32)


def cols_dot(left, right):
    return lax.dot_general(left, right, (((1,), (1,)), ((), ())), preferred_element_type=F32)


def side_parts(chunks, count):
    rows, width = chunks[0].shape
    part = width // (3 * count)

    def body(*refs):
        out = refs[-1]
        for at, chunk in enumerate(refs[:-1]):
            for third in range(3):
                for place in range(count):
                    begin = (third * count + place) * part
                    out[place, at * rows : (at + 1) * rows, third * part : (third + 1) * part] = (
                        chunk[:, begin : begin + part]
                    )

    shape = jax.ShapeDtypeStruct((count, len(chunks) * rows, 3 * part), chunks[0].dtype)
    spec = pl.BlockSpec(memory_space=pltpu.VMEM)
    return pl.pallas_call(
        body, out_shape=shape, in_specs=[spec] * len(chunks), out_specs=spec
    )(*chunks)


def step(acts, out_grad, params, moment, second):
    sections = lax.axis_size("pipe")
    section = lax.axis_index("pipe")
    places = lax.axis_size(DP)
    side = lax.axis_size(SIDE)
    width = acts.shape[-1]
    tokens = acts.shape[1] * acts.shape[2]
    rows = tokens // CHUNKS
    lead = sections - 1
    ticks = CHUNKS + DEPTH * lead
    first_chunk = (section * (DEPTH * rows)).astype(jnp.uint32)
    is_section = [section == at for at in range(sections)]
    acts, first_chunk, is_section = lax.optimization_barrier((acts, first_chunk, is_section))
    inputs = acts.reshape(-1, width)
    top = out_grad.reshape(-1, width)
    block = params.shape[1] // 3
    weights_in = params[0, : 2 * block]
    weights_down = params[0, 2 * block :]
    gate_up = cols_dot(inputs, weights_in)
    gate = gate_up[:, :block]
    up = gate_up[:, block:]
    sg = jax.nn.sigmoid(gate)
    activated = gate * sg
    factors = jnp.concatenate([up * sg * (1.0 + gate * (1.0 - sg)), activated], axis=1)
    hidden = (activated * up).astype(BF16)
    pad = jnp.zeros((DEPTH * lead * rows, 2 * block), F32)
    factors = lax.dynamic_slice(
        jnp.concatenate([pad, factors, pad], axis=0),
        (first_chunk, jnp.uint32(0)),
        (ticks * rows, 2 * block),
    )
    factors = lax.optimization_barrier(
        [factors[tick * rows : (tick + 1) * rows] for tick in range(ticks)]
    )
    copies = jnp.broadcast_to(hidden[None], (side,) + hidden.shape)
    hidden = lax.all_to_all(copies, SIDE, 0, 0, tiled=True)
    top = jnp.where(is_section[lead], top, 0)
    tops = lax.optimization_barrier(
        [top[chunk * rows : (chunk + 1) * rows] for chunk in range(CHUNKS)]
    )
    down = [(s, s - 1) for s in range(1, sections)]

    def own(values, count):
        chunks = []
        for chunk in range(count):
            value = values[chunk]
            for behind in range(1, sections):
                value = jnp.where(is_section[lead - behind], values[chunk + DEPTH * behind], value)
            chunks.append(value)
        return chunks

    moved = []
    grads = []
    passes = []
    parts = []
    for tick in range(ticks):
        grad = None if tick < DEPTH else moved[tick - DEPTH]
        if tick < CHUNKS:
            grad = tops[tick] if grad is None else grad + tops[tick]
        grads.append(grad)
        d_hidden = cols_dot(grad, weights_down)
        d_gate_up = jnp.concatenate([d_hidden, d_hidden], axis=1) * factors[tick]
        d_gate_up = d_gate_up.astype(BF16)
        passed = grad.astype(F32) + jnp.dot(d_gate_up, weights_in, preferred_element_type=F32)
        passed = passed.astype(BF16)
        passes.append(passed)
        if tick + DEPTH < ticks:
            moved.append(lax.ppermute(passed, "pipe", down))
        done = tick + 1 - DEPTH * lead
        if done == CHUNKS - DEPTH or done == CHUNKS:
            begin = len(parts)
            seen, _ = lax.optimization_barrier((grads[begin:], passed if begin == 0 else grad))
            parts += own(seen, done - begin)
    parts = side_parts(parts, side)
    arrived = lax.all_to_all(parts, SIDE, 0, 0, tiled=True)
    passes, arrived = lax.optimization_barrier((passes, arrived))
    terms = rows_dot(hidden.reshape(-1, block), arrived.reshape(-1, arrived.shape[2]))

    in_grads = jnp.concatenate(own(passes, CHUNKS), axis=0)

    terms = terms.astype(BF16).reshape(places, 2, -1)
    terms = lax.all_to_all(terms, DP, 0, 0, tiled=True)
    sizes = tuple(lax.axis_size(name) for name in DP)
    summed = jnp.sum(terms.astype(F32).reshape(sizes + terms.shape[1:]), axis=(1, 2))
    summed = summed.reshape(side, 4, -1).transpose(1, 0, 2).reshape(-1)

    gradient = summed * float(tokens * places) ** (-0.5)
    new_moment = 0.9 * moment[0] + 0.1 * gradient
    new_second = 0.999 * second[0] + 0.001 * gradient * gradient
    update = new_moment / (1.0 - 0.9**10) / (jnp.sqrt(new_second / (1.0 - 0.999**10)) + 1e-08)
    return (in_grads.reshape(acts.shape), new_moment[None], new_second[None], update[None])


def solution(mesh):
    fine = Mesh(mesh.devices.reshape(4, 2, 12, 2, 4), DP + ("pipe",))
    placed = (
        P("pipe", None, DP, None),
        P(None, DP, None),
        P("pipe", None, None),
        P("pipe", DP),
        P("pipe", DP),
    )
    return jax.shard_map(
        step,
        mesh=fine,
        in_specs=placed,
        out_specs=(P("pipe", None, DP, None), P("pipe", DP), P("pipe", DP), P("pipe", DP)),
        check_vma=False,
    )
```

```python
import jax
import jax.numpy as jnp
from jax import lax
from jax.experimental import pallas as pl
from jax.experimental.pallas import tpu as pltpu
from jax.sharding import Mesh, PartitionSpec as P


CHUNKS = 8
DEPTH = 2
DP = ("x", "yl", "z", "core")
SIDE = ("x", "core")
F32 = jnp.float32
BF16 = jnp.bfloat16


def rows_dot(left, right):
    return lax.dot_general(left, right, (((0,), (0,)), ((), ())), preferred_element_type=F32)


def cols_dot(left, right):
    return lax.dot_general(left, right, (((1,), (1,)), ((), ())), preferred_element_type=F32)


def side_parts(chunks, count):
    rows, width = chunks[0].shape
    part = width // (3 * count)

    def body(*refs):
        out = refs[-1]
        for at, chunk in enumerate(refs[:-1]):
            for third in range(3):
                for place in range(count):
                    begin = (third * count + place) * part
                    out[place, at * rows : (at + 1) * rows, third * part : (third + 1) * part] = (
                        chunk[:, begin : begin + part]
                    )

    shape = jax.ShapeDtypeStruct((count, len(chunks) * rows, 3 * part), chunks[0].dtype)
    spec = pl.BlockSpec(memory_space=pltpu.VMEM)
    return pl.pallas_call(
        body, out_shape=shape, in_specs=[spec] * len(chunks), out_specs=spec
    )(*chunks)


def step(acts, out_grad, params, moment, second):
    sections = lax.axis_size("pipe")
    section = lax.axis_index("pipe")
    places = lax.axis_size(DP)
    side = lax.axis_size(SIDE)
    width = acts.shape[-1]
    tokens = acts.shape[1] * acts.shape[2]
    rows = tokens // CHUNKS
    lead = sections - 1
    ticks = CHUNKS + DEPTH * lead
    first_chunk = (section * (DEPTH * rows)).astype(jnp.uint32)
    is_section = [section == at for at in range(sections)]
    acts, first_chunk, is_section = lax.optimization_barrier((acts, first_chunk, is_section))
    inputs = acts.reshape(-1, width)
    top = out_grad.reshape(-1, width)
    block = params.shape[1] // 3
    weights_in = params[0, : 2 * block]
    weights_down = params[0, 2 * block :]
    gate_up = cols_dot(inputs, weights_in)
    gate = gate_up[:, :block]
    up = gate_up[:, block:]
    sg = jax.nn.sigmoid(gate)
    activated = gate * sg
    factors = jnp.concatenate([up * sg * (1.0 + gate * (1.0 - sg)), activated], axis=1)
    hidden = (activated * up).astype(BF16)
    pad = jnp.zeros((DEPTH * lead * rows, 2 * block), F32)
    factors = lax.dynamic_slice(
        jnp.concatenate([pad, factors, pad], axis=0),
        (first_chunk, jnp.uint32(0)),
        (ticks * rows, 2 * block),
    )
    factors = lax.optimization_barrier(
        [factors[tick * rows : (tick + 1) * rows] for tick in range(ticks)]
    )
    copies = jnp.broadcast_to(hidden[None], (side,) + hidden.shape)
    hidden = lax.all_to_all(copies, SIDE, 0, 0, tiled=True)
    top = jnp.where(is_section[lead], top, 0)
    tops = lax.optimization_barrier(
        [top[chunk * rows : (chunk + 1) * rows] for chunk in range(CHUNKS)]
    )

    def own(values, count):
        chunks = []
        for chunk in range(count):
            value = values[chunk]
            for behind in range(1, sections):
                value = jnp.where(is_section[lead - behind], values[chunk + DEPTH * behind], value)
            chunks.append(value)
        return chunks

    moved = []
    grads = []
    passes = []
    parts = []
    for tick in range(ticks):
        grad = None if tick < DEPTH else moved[tick - DEPTH]
        if tick < CHUNKS:
            grad = tops[tick] if grad is None else grad + tops[tick]
        grads.append(grad)
        d_hidden = cols_dot(grad, weights_down)
        d_gate_up = jnp.concatenate([d_hidden, d_hidden], axis=1) * factors[tick]
        d_gate_up = d_gate_up.astype(BF16)
        passed = grad.astype(F32) + jnp.dot(d_gate_up, weights_in, preferred_element_type=F32)
        passed = passed.astype(BF16)
        passes.append(passed)
        if tick + DEPTH < ticks:
            down = [
                (s, s - 1)
                for s in range(1, sections)
                if 0 <= tick - DEPTH * (lead - s) < CHUNKS
            ]
            moved.append(lax.ppermute(passed, "pipe", down))
        done = tick + 1 - DEPTH * lead
        if done == CHUNKS - DEPTH or done == CHUNKS:
            begin = len(parts)
            seen, _ = lax.optimization_barrier((grads[begin:], passed if begin == 0 else grad))
            parts += own(seen, done - begin)
    parts = side_parts(parts, side)
    arrived = lax.all_to_all(parts, SIDE, 0, 0, tiled=True)
    passes, arrived = lax.optimization_barrier((passes, arrived))
    terms = rows_dot(hidden.reshape(-1, block), arrived.reshape(-1, arrived.shape[2]))

    in_grads = jnp.concatenate(own(passes, CHUNKS), axis=0)

    terms = terms.astype(BF16).reshape(places, 2, -1)
    terms = lax.all_to_all(terms, DP, 0, 0, tiled=True)
    sizes = tuple(lax.axis_size(name) for name in DP)
    summed = jnp.sum(terms.astype(F32).reshape(sizes + terms.shape[1:]), axis=(1, 2))
    summed = summed.reshape(side, 4, -1).transpose(1, 0, 2).reshape(moment.shape)
    summed = lax.optimization_barrier(summed)

    gradient = summed * float(tokens * places) ** (-0.5)
    new_moment = 0.9 * moment + 0.1 * gradient
    new_second = 0.999 * second + 0.001 * gradient * gradient
    update = new_moment / (1.0 - 0.9**10) / (jnp.sqrt(new_second / (1.0 - 0.999**10)) + 1e-08)
    return (in_grads.reshape(acts.shape), new_moment, new_second, update)


def solution(mesh):
    fine = Mesh(mesh.devices.reshape(4, 2, 12, 2, 4), DP + ("pipe",))
    placed = (
        P("pipe", None, DP, None),
        P(None, DP, None),
        P("pipe", None, None),
        P("pipe", DP),
        P("pipe", DP),
    )
    return jax.shard_map(
        step,
        mesh=fine,
        in_specs=placed,
        out_specs=(P("pipe", None, DP, None), P("pipe", DP), P("pipe", DP), P("pipe", DP)),
        check_vma=False,
    )
```

```python
import jax
import jax.numpy as jnp
from jax import lax
from jax.experimental import pallas as pl
from jax.experimental.pallas import tpu as pltpu
from jax.sharding import Mesh, PartitionSpec as P


CHUNKS = 8
DEPTH = 2
DP = ("x", "yl", "z", "core")
SIDE = ("x", "core")
F32 = jnp.float32
BF16 = jnp.bfloat16


def rows_dot(left, right):
    return lax.dot_general(left, right, (((0,), (0,)), ((), ())), preferred_element_type=F32)


def cols_dot(left, right):
    return lax.dot_general(left, right, (((1,), (1,)), ((), ())), preferred_element_type=F32)


def side_parts(chunks, count):
    rows, width = chunks[0].shape
    third = width // 3
    part = third // count

    def body(*refs):
        out = refs[-1]
        for at in range(3):
            span = slice(at * third, (at + 1) * third)
            turned = jnp.concatenate([chunk[:, span] for chunk in refs[:-1]], axis=0).T
            for place in range(count):
                out[place, at * part : (at + 1) * part, :] = (
                    turned[place * part : (place + 1) * part]
                )

    shape = jax.ShapeDtypeStruct((count, 3 * part, len(chunks) * rows), chunks[0].dtype)
    spec = pl.BlockSpec(memory_space=pltpu.VMEM)
    return pl.pallas_call(
        body, out_shape=shape, in_specs=[spec] * len(chunks), out_specs=spec
    )(*chunks)


def step(acts, out_grad, params, moment, second):
    sections = lax.axis_size("pipe")
    section = lax.axis_index("pipe")
    places = lax.axis_size(DP)
    side = lax.axis_size(SIDE)
    width = acts.shape[-1]
    tokens = acts.shape[1] * acts.shape[2]
    rows = tokens // CHUNKS
    lead = sections - 1
    ticks = CHUNKS + DEPTH * lead
    first_chunk = (section * (DEPTH * rows)).astype(jnp.uint32)
    is_section = [section == at for at in range(sections)]
    acts, first_chunk, is_section = lax.optimization_barrier((acts, first_chunk, is_section))
    inputs = acts.reshape(-1, width)
    top = out_grad.reshape(-1, width)
    block = params.shape[1] // 3
    weights_in = params[0, : 2 * block]
    weights_down = params[0, 2 * block :]
    gate_up = cols_dot(inputs, weights_in)
    gate = gate_up[:, :block]
    up = gate_up[:, block:]
    sg = jax.nn.sigmoid(gate)
    activated = gate * sg
    factors = jnp.concatenate([up * sg * (1.0 + gate * (1.0 - sg)), activated], axis=1)
    hidden = (activated * up).astype(BF16)
    pad = jnp.zeros((DEPTH * lead * rows, 2 * block), F32)
    factors = lax.dynamic_slice(
        jnp.concatenate([pad, factors, pad], axis=0),
        (first_chunk, jnp.uint32(0)),
        (ticks * rows, 2 * block),
    )
    factors = lax.optimization_barrier(
        [factors[tick * rows : (tick + 1) * rows] for tick in range(ticks)]
    )
    copies = jnp.broadcast_to(hidden[None], (side,) + hidden.shape)
    hidden = lax.all_to_all(copies, SIDE, 0, 0, tiled=True)
    top = jnp.where(is_section[lead], top, 0)
    tops = lax.optimization_barrier(
        [top[chunk * rows : (chunk + 1) * rows] for chunk in range(CHUNKS)]
    )

    def own(values, count):
        chunks = []
        for chunk in range(count):
            value = values[chunk]
            for behind in range(1, sections):
                value = jnp.where(is_section[lead - behind], values[chunk + DEPTH * behind], value)
            chunks.append(value)
        return chunks

    moved = []
    grads = []
    passes = []
    parts = []
    for tick in range(ticks):
        grad = None if tick < DEPTH else moved[tick - DEPTH]
        if tick < CHUNKS:
            grad = tops[tick] if grad is None else grad + tops[tick]
        grads.append(grad)
        d_hidden = cols_dot(grad, weights_down)
        d_gate_up = jnp.concatenate([d_hidden, d_hidden], axis=1) * factors[tick]
        d_gate_up = d_gate_up.astype(BF16)
        passed = grad.astype(F32) + jnp.dot(d_gate_up, weights_in, preferred_element_type=F32)
        passed = passed.astype(BF16)
        passes.append(passed)
        if tick + DEPTH < ticks:
            down = [
                (s, s - 1)
                for s in range(1, sections)
                if 0 <= tick - DEPTH * (lead - s) < CHUNKS
            ]
            moved.append(lax.ppermute(passed, "pipe", down))
        done = tick + 1 - DEPTH * lead
        if done == CHUNKS - DEPTH or done == CHUNKS:
            begin = len(parts)
            seen, _ = lax.optimization_barrier((grads[begin:], passed if begin == 0 else grad))
            parts += own(seen, done - begin)
    parts = side_parts(parts, side)
    arrived = lax.all_to_all(parts, SIDE, 0, 0, tiled=True)
    passes, arrived = lax.optimization_barrier((passes, arrived))
    arrived = arrived.transpose(0, 2, 1)
    terms = rows_dot(hidden.reshape(-1, block), arrived.reshape(-1, arrived.shape[2]))

    in_grads = jnp.concatenate(own(passes, CHUNKS), axis=0)

    terms = terms.astype(BF16).reshape(places, 2, -1)
    terms = lax.all_to_all(terms, DP, 0, 0, tiled=True)
    sizes = tuple(lax.axis_size(name) for name in DP)
    summed = jnp.sum(terms.astype(F32).reshape(sizes + terms.shape[1:]), axis=(1, 2))
    summed = summed.reshape(side, 4, -1).transpose(1, 0, 2).reshape(moment.shape)
    summed = lax.optimization_barrier(summed)

    gradient = summed * float(tokens * places) ** (-0.5)
    new_moment = 0.9 * moment + 0.1 * gradient
    new_second = 0.999 * second + 0.001 * gradient * gradient
    update = new_moment / (1.0 - 0.9**10) / (jnp.sqrt(new_second / (1.0 - 0.999**10)) + 1e-08)
    return (in_grads.reshape(acts.shape), new_moment, new_second, update)


def solution(mesh):
    fine = Mesh(mesh.devices.reshape(4, 2, 12, 2, 4), DP + ("pipe",))
    placed = (
        P("pipe", None, DP, None),
        P(None, DP, None),
        P("pipe", None, None),
        P("pipe", DP),
        P("pipe", DP),
    )
    return jax.shard_map(
        step,
        mesh=fine,
        in_specs=placed,
        out_specs=(P("pipe", None, DP, None), P("pipe", DP), P("pipe", DP), P("pipe", DP)),
        check_vma=False,
    )
```
